32 devices in a mesh: dp: 16 (over z, x, core), zero: 2 (over y).
Axes of the slice: x: 2, y: 2, z: 4, core: 2. Of those that a mesh axis runs over, the one named last changes fastest.
Arguments:
- tokens: bfloat16 [4096, 768], P(('dp', 'zero')), may hold values from -6 to 6
- cotangent: bfloat16 [4096, 768], P(('dp', 'zero')), may hold values from -6 to 6
- lengths: int32 [32], P(('dp', 'zero')), may hold values from 16 to 128, as said below
- master: float32 [3545856], P('zero'), may hold values from -4 to 4, as said below
- moment_one: float32 [3545856], P('zero'), may hold values from -0.06 to 0.06
- moment_two: float32 [3545856], P('zero'), may hold values from 1e-06 to 0.008
Outputs:
- out: bfloat16 [4096, 768], P(('dp', 'zero'))
- grad_tokens: bfloat16 [4096, 768], P(('dp', 'zero'))
- gradient: float32 [3545856], P('zero')
- new_master: float32 [3545856], P('zero')
- new_moment_one: float32 [3545856], P('zero')
- new_moment_two: float32 [3545856], P('zero')
The draws below stay inside these ranges and needn't reach their ends.
Inputs may be any that keep to these rules, and one draw needn't show every extreme that they name: `lengths`: keys at or past a sequence's length are masked; sequences whose index is a multiple of 4 have length 128. `master`: laid out as in the first step.
All inputs are finite; a program needn't handle non-finite values.
Results may differ from the reference program's by a relative error of at most 0.025.
Values may be sent and summed in bfloat16 or wider, within the bound.
No kernel may reach another device: no remote copies, remote signals or barrier semaphores. Data moves between devices by JAX's collectives and lax.ppermute only.
A program may use at most 192 MiB of HBM per device.

```python
import math
import jax
import jax.numpy as jnp
from jax import lax

D = 768
HEADS = 6
HD = 64
FF = 1536
LEN = 128
SEQS = 32
TOKENS = 4096
P_SIZE = 3545856


def draw_master(key, part):
    inner_width = HEADS * HD
    segment_specs = [(3 * D * inner_width, D ** (-0.5), 0.0), (2 * inner_width, 0.1, 0.0), (inner_width * D, math.sqrt(LEN / 2.0 / inner_width), 0.0), (D, 0.1, 0.0), (D, 0.1, 1.0), (D, 0.1, 0.0), (D * FF, D ** (-0.5), 0.0), (FF, 0.1, 0.0), (FF * D, FF ** (-0.5), 0.0), (D, 0.1, 0.0), (D, 0.1, 1.0), (D, 0.1, 0.0)]
    pieces = []
    for position, row_spec in enumerate(segment_specs):
        sub_key = jax.random.fold_in(key, position + 11)
        random_part = jnp.clip(jax.random.normal(sub_key, (row_spec[0],), jnp.float32), -6.0, 6.0)
        pieces.append(row_spec[2] + row_spec[1] * random_part)
    return jnp.concatenate(pieces).astype(jnp.float32)


def draw_moment_two(key, part):
    low_log = math.log(1e-06)
    high_log = math.log(0.002)
    exponent = jax.random.uniform(jax.random.fold_in(key, 29), (P_SIZE,), jnp.float32, low_log, high_log)
    return jnp.clip(jnp.exp(exponent), 1e-06, 0.008).astype(jnp.float32)


def draw_lengths(key, part):
    random_len = jax.random.randint(key, (SEQS,), LEN // 8, LEN + 1, dtype=jnp.int32)
    full_rows = jnp.arange(SEQS, dtype=jnp.int32) % 4 == 0
    return jnp.where(full_rows, LEN, random_len).astype(jnp.int32)


def block_levels(rng, dims, cuts, low, largest):
    loudness, own = 1.0, jax.random.fold_in(rng, 6)
    for dim, blocks in cuts:
        steps = jnp.exp(jax.random.uniform(jax.random.fold_in(own, dim), (blocks,), jnp.float32, low / len(cuts), largest / len(cuts)))
        loudness = loudness * jnp.repeat(steps, dims[dim] // blocks).reshape([-1 if axis == dim else 1 for axis in range(len(dims))])
    return loudness


def bell_draw(stream_key, shape, deviation, bound, cuts=(), held_as=jnp.bfloat16):
    values = deviation * jax.random.normal(stream_key, shape, jnp.float32)
    if cuts:
        values = values * block_levels(stream_key, shape, cuts, -0.22, 0.18)
    return jnp.clip(values, -bound, bound).astype(held_as)


def setup_inputs(seed: int = 0) -> dict:
    key_list = jax.random.split(jax.random.key(seed), 7)
    return {
        "tokens": bell_draw(key_list[0], (TOKENS, D), 1.0, 6.0, ((0, 32),)),
        "cotangent": bell_draw(key_list[1], (TOKENS, D), 1.0, 6.0, ((0, 32),)),
        "lengths": draw_lengths(jax.random.fold_in(key_list[6], 71), 0),
        "master": draw_master(jax.random.fold_in(key_list[6], 71), 0),
        "moment_one": bell_draw(key_list[4], (P_SIZE,), 0.01, 0.06, ((0, 2),), jnp.float32),
        "moment_two": draw_moment_two(jax.random.fold_in(key_list[6], 71), 0),
    }


ln_eps = 1e-06
beta_one = 0.9
beta_two = 0.999
adam_eps = 1e-08
learn_rate = 0.01
decay_rate = 0.01
adam_step = 3
inv_sqrt_two = 0.7071067811865476
inv_sqrt_tau = 0.3989422804014327

def param_shapes():
    inner_width = HEADS * HD
    return [(D, 3 * inner_width), (2 * inner_width,), (inner_width, D), (D,), (D,), (D,), (D, FF), (FF,), (FF, D), (D,), (D,), (D,)]

def unpack(flat_vec):
    pieces = []
    offset = 0
    for dim_list in param_shapes():
        amount = math.prod(dim_list)
        pieces.append(flat_vec[offset:offset + amount].reshape(dim_list))
        offset += amount
    return pieces

def pack(pieces):
    return jnp.concatenate([member.reshape(-1) for member in pieces])

def mix(form, left, right):
    return jnp.einsum(form, left.astype(jnp.float32), right.astype(jnp.float32))

def matrix_product(left, right):
    return jnp.dot(left, right, preferred_element_type=jnp.float32)

def gelu_exact(argument):
    return 0.5 * argument * (1.0 + lax.erf(argument * inv_sqrt_two))

def gelu_slope(argument):
    return 0.5 * (1.0 + lax.erf(argument * inv_sqrt_two)) + argument * jnp.exp(-0.5 * argument * argument) * inv_sqrt_tau

def layer_normalize(hidden, gain_vec, bias_vec):
    centre = hidden - lax.optimization_barrier(jnp.mean(hidden, axis=-1, keepdims=True))
    inv_std = lax.rsqrt(lax.optimization_barrier(jnp.mean(centre * centre, axis=-1, keepdims=True)) + ln_eps)
    normed = centre * inv_std
    return (normed * gain_vec.astype(jnp.float32) + bias_vec.astype(jnp.float32), normed, inv_std)

def layer_normalize_backward(grad_in, normed, inv_std, gain_vec):
    scaled = grad_in * gain_vec.astype(jnp.float32)
    return inv_std * (scaled - lax.optimization_barrier(jnp.mean(scaled, axis=-1, keepdims=True)) - normed * lax.optimization_barrier(jnp.mean(scaled * normed, axis=-1, keepdims=True)))

def forward(tokens, lengths, weight_list):
    w_qkv, b_qv, w_out, b_out, first_norm_gain, first_norm_bias, w_up, b_up, w_down, b_down, second_norm_gain, second_norm_bias = weight_list
    scale_factor = 1.0 / math.sqrt(HD)
    seq_count = lengths.shape[0]
    inner_width = w_out.shape[0]
    head_count = inner_width // HD
    seq_len = tokens.shape[0] // seq_count
    projected = matrix_product(tokens, w_qkv)
    bias_full = jnp.concatenate([b_qv[:inner_width], jnp.zeros((inner_width,), b_qv.dtype), b_qv[inner_width:]]).astype(jnp.float32)
    projected = (projected + bias_full).astype(jnp.bfloat16).reshape(seq_count, seq_len, 3, head_count, HD)
    query_matrix = projected[:, :, 0]
    key_matrix = projected[:, :, 1]
    value_matrix = projected[:, :, 2]
    key_valid_mask = (jnp.arange(seq_len, dtype=jnp.int32)[None, :] < lengths.astype(jnp.int32)[:, None])[:, None, None, :]
    scores = mix('sqhe,skhe->shqk', query_matrix, key_matrix) * scale_factor
    exp_scores = jnp.where(key_valid_mask, jnp.exp(scores), 0.0)
    row_total = lax.optimization_barrier(jnp.sum(exp_scores, axis=-1, keepdims=True))
    logsumexp_total = jnp.log(row_total)
    attention_weights = (exp_scores / row_total).astype(jnp.bfloat16)
    attended_rows = mix('shqk,skhe->sqhe', attention_weights, value_matrix).astype(jnp.bfloat16).reshape(-1, inner_width)
    first_hidden_rows = tokens.astype(jnp.float32) + matrix_product(attended_rows, w_out) + b_out.astype(jnp.float32)
    first_normed_rows, first_centred_scaled, first_inverse_deviation = layer_normalize(first_hidden_rows, first_norm_gain, first_norm_bias)
    normed_halfprec = first_normed_rows.astype(jnp.bfloat16)
    preactivation_rows = matrix_product(normed_halfprec, w_up) + b_up.astype(jnp.float32)
    activation_halfprec = gelu_exact(preactivation_rows).astype(jnp.bfloat16)
    second_hidden_rows = normed_halfprec.astype(jnp.float32) + matrix_product(activation_halfprec, w_down) + b_down.astype(jnp.float32)
    second_normed_rows, second_centred_scaled, second_inverse_deviation = layer_normalize(second_hidden_rows, second_norm_gain, second_norm_bias)
    residuals_kept = (query_matrix, key_matrix, value_matrix, logsumexp_total, attention_weights, attended_rows, first_centred_scaled, first_inverse_deviation, normed_halfprec, preactivation_rows, activation_halfprec, second_centred_scaled, second_inverse_deviation, key_valid_mask)
    return (second_normed_rows.astype(jnp.bfloat16), residuals_kept)

def backward(cotangent, tokens, weight_list, residuals_kept):
    w_qkv, b_qv, w_out, b_out, first_norm_gain, first_norm_bias, w_up, b_up, w_down, b_down, second_norm_gain, second_norm_bias = weight_list
    query_matrix, key_matrix, value_matrix, logsumexp_total, attention_weights, attended_rows, first_centred_scaled, first_inverse_deviation, normed_halfprec, preactivation_rows, activation_halfprec, second_centred_scaled, second_inverse_deviation, key_valid_mask = residuals_kept
    scale_factor = 1.0 / math.sqrt(HD)
    output_gradient = cotangent.astype(jnp.float32)
    second_hidden_gradient = layer_normalize_backward(output_gradient, second_centred_scaled, second_inverse_deviation, second_norm_gain)
    second_hidden_halfprec = second_hidden_gradient.astype(jnp.bfloat16)
    preactivation_gradient = matrix_product(second_hidden_halfprec, w_down.T) * gelu_slope(preactivation_rows)
    preactivation_halfprec = preactivation_gradient.astype(jnp.bfloat16)
    first_normed_gradient = second_hidden_gradient + matrix_product(preactivation_halfprec, w_up.T)
    first_hidden_gradient = layer_normalize_backward(first_normed_gradient, first_centred_scaled, first_inverse_deviation, first_norm_gain)
    first_hidden_halfprec = first_hidden_gradient.astype(jnp.bfloat16)
    seq_count, seq_len, head_count = (query_matrix.shape[0], query_matrix.shape[1], query_matrix.shape[2])
    inner_width = head_count * HD
    grad_context = matrix_product(first_hidden_halfprec, w_out.T).astype(jnp.bfloat16).reshape(seq_count, seq_len, head_count, HD)
    scores = mix('sqhe,skhe->shqk', query_matrix, key_matrix) * scale_factor
    exact_probs = jnp.where(key_valid_mask, jnp.exp(scores - logsumexp_total), 0.0)
    grad_probs = mix('sqhe,skhe->shqk', grad_context, value_matrix)
    row_inner = lax.optimization_barrier(jnp.sum(exact_probs * grad_probs, axis=-1, keepdims=True))
    grad_scores = (exact_probs * (grad_probs - row_inner) * scale_factor).astype(jnp.bfloat16)
    grad_queries = mix('shqk,skhe->sqhe', grad_scores, key_matrix)
    grad_keys = mix('shqk,sqhe->skhe', grad_scores, query_matrix)
    grad_values = mix('shqk,sqhe->skhe', attention_weights, grad_context)
    projection_gradient = jnp.stack([grad_queries, grad_keys, grad_values], axis=2).astype(jnp.bfloat16).reshape(-1, 3 * inner_width)
    grad_tokens = (first_hidden_gradient + matrix_product(projection_gradient, w_qkv.T)).astype(jnp.bfloat16)
    query_value_bias_gradient = jnp.concatenate([lax.optimization_barrier(jnp.sum(grad_queries.reshape(-1, inner_width), axis=0)), lax.optimization_barrier(jnp.sum(grad_values.reshape(-1, inner_width), axis=0))])
    gradient_listing = [matrix_product(tokens.T, projection_gradient), query_value_bias_gradient, matrix_product(attended_rows.T, first_hidden_halfprec), lax.optimization_barrier(jnp.sum(first_hidden_gradient, axis=0)), lax.optimization_barrier(jnp.sum(first_normed_gradient * first_centred_scaled, axis=0)), lax.optimization_barrier(jnp.sum(first_normed_gradient, axis=0)), matrix_product(normed_halfprec.T, preactivation_halfprec), lax.optimization_barrier(jnp.sum(preactivation_gradient, axis=0)), matrix_product(activation_halfprec.T, second_hidden_halfprec), lax.optimization_barrier(jnp.sum(second_hidden_gradient, axis=0)), lax.optimization_barrier(jnp.sum(output_gradient * second_centred_scaled, axis=0)), lax.optimization_barrier(jnp.sum(output_gradient, axis=0))]
    return (gradient_listing, grad_tokens)

def reference(tokens, cotangent, lengths, master, moment_one, moment_two):
    weight_list = unpack(master.astype(jnp.bfloat16))
    block_seqs = math.gcd(SEQS, max(1, 4096 // LEN))
    block_count = SEQS // block_seqs
    tok_blocks = tokens.reshape(block_count, block_seqs * LEN, D)
    cot_blocks = cotangent.reshape(block_count, block_seqs * LEN, D)
    len_blocks = lengths.reshape(block_count, block_seqs)

    def block_step(running, inputs):
        tok_block, cot_block, len_block = inputs
        out_block, residuals_kept = forward(tok_block, len_block, weight_list)
        gradient_listing, grad_block = backward(cot_block, tok_block, weight_list, residuals_kept)
        return (running + pack(gradient_listing), (out_block, grad_block))
    summed, (out_rows, grad_rows) = lax.scan(block_step, jnp.zeros((P_SIZE,), jnp.float32), (tok_blocks, cot_blocks, len_blocks))
    gradient = summed * (1.0 / SEQS)
    corr_one = 1.0 - beta_one ** adam_step
    corr_two = 1.0 - beta_two ** adam_step
    moment_new = beta_one * moment_one + (1.0 - beta_one) * gradient
    second_new = beta_two * moment_two + (1.0 - beta_two) * gradient * gradient
    step_dir = moment_new / corr_one / (jnp.sqrt(second_new / corr_two) + adam_eps)
    master_new = master - learn_rate * (step_dir + decay_rate * master)
    return (out_rows.reshape(TOKENS, D), grad_rows.reshape(TOKENS, D), gradient, master_new, moment_new, second_new)
```

```python
import math
from functools import partial

import jax
import jax.numpy as jnp
from jax import lax
from jax.experimental import pallas as pl
from jax.experimental.pallas import tpu as pltpu
from jax.sharding import PartitionSpec as P

D = 768
HEADS = 6
HD = 64
FF = 1536


ln_eps = 1e-06
beta_one = 0.9
beta_two = 0.999
adam_eps = 1e-08
learn_rate = 0.01
decay_rate = 0.01
adam_step = 3
inv_sqrt_two = 0.7071067811865476
inv_sqrt_tau = 0.3989422804014327


def param_shapes():
    inner_width = HEADS * HD
    return [
        (D, 3 * inner_width),
        (2 * inner_width,),
        (inner_width, D),
        (D,),
        (D,),
        (D,),
        (D, FF),
        (FF,),
        (FF, D),
        (D,),
        (D,),
        (D,),
    ]


def unpack(flat_vec):
    pieces = []
    offset = 0
    for dim_list in param_shapes():
        amount = math.prod(dim_list)
        pieces.append(flat_vec[offset : offset + amount].reshape(dim_list))
        offset += amount
    return pieces


def pack(pieces):
    return jnp.concatenate([member.reshape(-1) for member in pieces])


def mix(form, left, right):
    return jnp.einsum(form, left, right, preferred_element_type=jnp.float32)


def matrix_product(left, right):
    return jnp.dot(left, right, preferred_element_type=jnp.float32)


def gelu_exact(argument):
    return 0.5 * argument * (1.0 + lax.erf(argument * inv_sqrt_two))


def gelu_slope(argument):
    return (
        0.5 * (1.0 + lax.erf(argument * inv_sqrt_two))
        + argument * jnp.exp(-0.5 * argument * argument) * inv_sqrt_tau
    )


def layer_normalize(hidden, gain_vec, bias_vec):
    centre = hidden - jnp.mean(hidden, axis=-1, keepdims=True)
    inv_std = lax.rsqrt(jnp.mean(centre * centre, axis=-1, keepdims=True) + ln_eps)
    normed = centre * inv_std
    return (normed * gain_vec.astype(jnp.float32) + bias_vec.astype(jnp.float32), normed, inv_std)


def layer_normalize_backward(grad_in, normed, inv_std, gain_vec):
    scaled = grad_in * gain_vec.astype(jnp.float32)
    return inv_std * (
        scaled
        - jnp.mean(scaled, axis=-1, keepdims=True)
        - normed * jnp.mean(scaled * normed, axis=-1, keepdims=True)
    )


def forward(tokens, lengths, weight_list):
    (
        w_qkv,
        b_qv,
        w_out,
        b_out,
        first_norm_gain,
        first_norm_bias,
        w_up,
        b_up,
        w_down,
        b_down,
        second_norm_gain,
        second_norm_bias,
    ) = weight_list
    scale_factor = 1.0 / math.sqrt(HD)
    seq_count = lengths.shape[0]
    inner_width = w_out.shape[0]
    head_count = inner_width // HD
    seq_len = tokens.shape[0] // seq_count
    projected = matrix_product(tokens, w_qkv)
    bias_full = jnp.concatenate(
        [b_qv[:inner_width], jnp.zeros((inner_width,), jnp.bfloat16), b_qv[inner_width:]]
    ).astype(jnp.float32)
    projected = (
        (projected + bias_full).astype(jnp.bfloat16).reshape(seq_count, seq_len, 3, head_count, HD)
    )
    query_matrix = projected[:, :, 0]
    key_matrix = projected[:, :, 1]
    value_matrix = projected[:, :, 2]
    key_valid_mask = (jnp.arange(seq_len, dtype=jnp.int32)[None, :] < lengths[:, None])[
        :, None, None, :
    ]
    scores = mix("sqhe,skhe->shqk", query_matrix, key_matrix) * scale_factor
    exp_scores = jnp.where(key_valid_mask, jnp.exp(scores), 0.0)
    row_total = jnp.sum(exp_scores, axis=-1, keepdims=True)
    logsumexp_total = jnp.log(row_total)
    attention_weights = (exp_scores / row_total).astype(jnp.bfloat16)
    attended_rows = (
        mix("shqk,skhe->sqhe", attention_weights, value_matrix)
        .astype(jnp.bfloat16)
        .reshape(-1, inner_width)
    )
    first_hidden_rows = (
        tokens.astype(jnp.float32)
        + matrix_product(attended_rows, w_out)
        + b_out.astype(jnp.float32)
    )
    first_normed_rows, first_centred_scaled, first_inverse_deviation = layer_normalize(
        first_hidden_rows, first_norm_gain, first_norm_bias
    )
    normed_halfprec = first_normed_rows.astype(jnp.bfloat16)
    preactivation_rows = matrix_product(normed_halfprec, w_up) + b_up.astype(jnp.float32)
    activation_halfprec = gelu_exact(preactivation_rows).astype(jnp.bfloat16)
    second_hidden_rows = (
        normed_halfprec.astype(jnp.float32)
        + matrix_product(activation_halfprec, w_down)
        + b_down.astype(jnp.float32)
    )
    second_normed_rows, second_centred_scaled, second_inverse_deviation = layer_normalize(
        second_hidden_rows, second_norm_gain, second_norm_bias
    )
    residuals_kept = (
        query_matrix,
        key_matrix,
        value_matrix,
        logsumexp_total,
        attention_weights,
        attended_rows,
        first_centred_scaled,
        first_inverse_deviation,
        normed_halfprec,
        preactivation_rows,
        activation_halfprec,
        second_centred_scaled,
        second_inverse_deviation,
        key_valid_mask,
    )
    return (second_normed_rows.astype(jnp.bfloat16), residuals_kept)


def backward(cotangent, tokens, weight_list, residuals_kept):
    (
        w_qkv,
        b_qv,
        w_out,
        b_out,
        first_norm_gain,
        first_norm_bias,
        w_up,
        b_up,
        w_down,
        b_down,
        second_norm_gain,
        second_norm_bias,
    ) = weight_list
    (
        query_matrix,
        key_matrix,
        value_matrix,
        logsumexp_total,
        attention_weights,
        attended_rows,
        first_centred_scaled,
        first_inverse_deviation,
        normed_halfprec,
        preactivation_rows,
        activation_halfprec,
        second_centred_scaled,
        second_inverse_deviation,
        key_valid_mask,
    ) = residuals_kept
    scale_factor = 1.0 / math.sqrt(HD)
    output_gradient = cotangent.astype(jnp.float32)
    second_hidden_gradient = layer_normalize_backward(
        output_gradient, second_centred_scaled, second_inverse_deviation, second_norm_gain
    )
    second_hidden_halfprec = second_hidden_gradient.astype(jnp.bfloat16)
    preactivation_gradient = matrix_product(second_hidden_halfprec, w_down.T) * gelu_slope(
        preactivation_rows
    )
    preactivation_halfprec = preactivation_gradient.astype(jnp.bfloat16)
    first_normed_gradient = second_hidden_gradient + matrix_product(preactivation_halfprec, w_up.T)
    first_hidden_gradient = layer_normalize_backward(
        first_normed_gradient, first_centred_scaled, first_inverse_deviation, first_norm_gain
    )
    first_hidden_halfprec = first_hidden_gradient.astype(jnp.bfloat16)
    seq_count, seq_len, head_count = (
        query_matrix.shape[0],
        query_matrix.shape[1],
        query_matrix.shape[2],
    )
    inner_width = head_count * HD
    grad_context = (
        matrix_product(first_hidden_halfprec, w_out.T)
        .astype(jnp.bfloat16)
        .reshape(seq_count, seq_len, head_count, HD)
    )
    scores = mix("sqhe,skhe->shqk", query_matrix, key_matrix) * scale_factor
    exact_probs = jnp.where(key_valid_mask, jnp.exp(scores - logsumexp_total), 0.0)
    grad_probs = mix("sqhe,skhe->shqk", grad_context, value_matrix)
    row_inner = jnp.sum(exact_probs * grad_probs, axis=-1, keepdims=True)
    grad_scores = (exact_probs * (grad_probs - row_inner) * scale_factor).astype(jnp.bfloat16)
    grad_queries = mix("shqk,skhe->sqhe", grad_scores, key_matrix)
    grad_keys = mix("shqk,sqhe->skhe", grad_scores, query_matrix)
    grad_values = mix("shqk,sqhe->skhe", attention_weights, grad_context)
    projection_gradient = (
        jnp.stack([grad_queries, grad_keys, grad_values], axis=2)
        .astype(jnp.bfloat16)
        .reshape(-1, 3 * inner_width)
    )
    grad_tokens = (first_hidden_gradient + matrix_product(projection_gradient, w_qkv.T)).astype(
        jnp.bfloat16
    )
    query_value_bias_gradient = jnp.concatenate(
        [
            jnp.sum(grad_queries.reshape(-1, inner_width), axis=0),
            jnp.sum(grad_values.reshape(-1, inner_width), axis=0),
        ]
    )
    gradient_listing = [
        matrix_product(tokens.T, projection_gradient),
        query_value_bias_gradient,
        matrix_product(attended_rows.T, first_hidden_halfprec),
        jnp.sum(first_hidden_gradient, axis=0),
        jnp.sum(first_normed_gradient * first_centred_scaled, axis=0),
        jnp.sum(first_normed_gradient, axis=0),
        matrix_product(normed_halfprec.T, preactivation_halfprec),
        jnp.sum(preactivation_gradient, axis=0),
        matrix_product(activation_halfprec.T, second_hidden_halfprec),
        jnp.sum(second_hidden_gradient, axis=0),
        jnp.sum(output_gradient * second_centred_scaled, axis=0),
        jnp.sum(output_gradient, axis=0),
    ]
    return (gradient_listing, grad_tokens)


def per_device_general(tokens, cotangent, lengths, master, moment_one, moment_two):
    local_half = master.astype(jnp.bfloat16)
    gathered = lax.all_gather(local_half, "zero", axis=0, tiled=True)
    weight_list = unpack(gathered)
    out_rows, residuals_kept = forward(tokens, lengths, weight_list)
    gradient_listing, grad_tokens = backward(cotangent, tokens, weight_list, residuals_kept)
    dp_count = lax.axis_size("dp")
    zero_count = lax.axis_size("zero")
    seq_total = lengths.shape[0] * dp_count * zero_count
    local_grad = pack(gradient_listing)
    owner_part = lax.psum_scatter(
        local_grad.astype(jnp.bfloat16), "zero", scatter_dimension=0, tiled=True
    )
    piece_sum = lax.psum_scatter(owner_part, "dp", scatter_dimension=0, tiled=True).astype(
        jnp.float32
    )
    summed = lax.all_gather(piece_sum.astype(jnp.bfloat16), "dp", axis=0, tiled=True).astype(
        piece_sum.dtype
    )
    gradient = summed * (1.0 / seq_total)
    corr_one = 1.0 - beta_one**adam_step
    corr_two = 1.0 - beta_two**adam_step
    moment_new = beta_one * moment_one + (1.0 - beta_one) * gradient
    second_new = beta_two * moment_two + (1.0 - beta_two) * gradient * gradient
    step_dir = moment_new / corr_one / (jnp.sqrt(second_new / corr_two) + adam_eps)
    master_new = master - learn_rate * (step_dir + decay_rate * master)
    return (out_rows, grad_tokens, gradient, master_new, moment_new, second_new)


LANE = 128
INNER = HEADS * HD
BF = jnp.bfloat16
F32 = jnp.float32
VMEM = pltpu.MemorySpace.VMEM
SMEM = pltpu.MemorySpace.SMEM
ANY = pl.ANY
CHUNKS = 3


def lines(amount):
    return amount // LANE


QKV_N = lines(3 * INNER)
UP_N = lines(FF)
DIM_N = lines(D)
AT_BQV = lines(D * 3 * INNER)
AT_OUT = AT_BQV + lines(2 * INNER)
AT_BOUT = AT_OUT + lines(INNER * D)
AT_GONE = AT_BOUT + DIM_N
AT_BONE = AT_GONE + DIM_N
AT_UP = AT_BONE + DIM_N
AT_BUP = AT_UP + lines(D * FF)
AT_DOWN = AT_BUP + UP_N
AT_BDOWN = AT_DOWN + lines(FF * D)
AT_GTWO = AT_BDOWN + DIM_N
AT_BTWO = AT_GTWO + DIM_N
TOTAL = AT_BTWO + DIM_N
HALF = TOTAL // 2
UP_LOW = HALF - AT_UP
UP_HIGH = AT_BUP - HALF
SHARE = -(-UP_LOW // 16) * 8


def call(kernel, outs, scratch=(), grid=None, vmem=56, **more):
    return pl.pallas_call(
        kernel,
        out_shape=outs,
        scratch_shapes=list(scratch),
        compiler_params=pltpu.CompilerParams(vmem_limit_bytes=vmem * 1024 * 1024),
        **more,
    )


def shaped(rows, cols, kind):
    return jax.ShapeDtypeStruct((rows, cols), kind)


def vm(count):
    return [pl.BlockSpec(memory_space=VMEM)] * count


SCALARS = pl.BlockSpec(memory_space=SMEM)
WHOLE = pl.BlockSpec(memory_space=ANY)


def rounded(block):
    return block.astype(BF).astype(F32)


def put_vector(target, row, source, first, count, start=0):
    for piece in range(count):
        target[row : row + 1, (start + piece) * LANE : (start + piece + 1) * LANE] = rounded(
            source[first + piece : first + piece + 1, :]
        )


def prepare_kernel(ids, master, main, send, vec, flat, sem):
    copy = pltpu.make_async_copy(master, flat, sem)
    copy.start()
    copy.wait()

    @pl.when(ids[0] == 0)
    def _():
        for j in range(QKV_N):
            main[j * D : (j + 1) * D, :] = flat[pl.ds(j, D, stride=QKV_N), :].astype(BF)
        for j in range(DIM_N):
            base = QKV_N * D + j * INNER
            main[base : base + INNER, :] = flat[pl.ds(AT_OUT + j, INNER, stride=DIM_N), :].astype(BF)
        inner_n = lines(INNER)
        vec[0:1, INNER : 2 * INNER] = jnp.zeros((1, INNER), F32)
        put_vector(vec, 0, flat, AT_BQV, inner_n)
        put_vector(vec, 0, flat, AT_BQV + inner_n, inner_n, 2 * inner_n)
        put_vector(vec, 1, flat, AT_BOUT, DIM_N)
        put_vector(vec, 2, flat, AT_GONE, DIM_N)
        put_vector(vec, 3, flat, AT_BONE, DIM_N)

        @pl.when(ids[2] == 0)
        def _():
            send[...] = flat[AT_UP : AT_UP + SHARE, :].astype(BF)

        @pl.when(ids[2] != 0)
        def _():
            send[...] = flat[HALF - SHARE : HALF, :].astype(BF)

    @pl.when(ids[0] != 0)
    def _():
        for j in range(DIM_N):
            main[j * FF : (j + 1) * FF, :] = flat[
                pl.ds(AT_DOWN - HALF + j, FF, stride=DIM_N), :
            ].astype(BF)
        put_vector(vec, 0, flat, AT_BUP - HALF, UP_N)
        put_vector(vec, 1, flat, AT_BDOWN - HALF, DIM_N)
        put_vector(vec, 2, flat, AT_GTWO - HALF, DIM_N)
        put_vector(vec, 3, flat, AT_BTWO - HALF, DIM_N)


def prepare(ids, master):
    return call(
        prepare_kernel,
        (shaped(D * UP_N, LANE, BF), shaped(SHARE, LANE, BF), shaped(8, FF, F32)),
        (pltpu.VMEM((HALF, LANE), F32), pltpu.SemaphoreType.DMA),
        in_specs=[SCALARS, WHOLE],
        out_specs=tuple(vm(3)),
        name="prepare",
    )(ids, master)


def join_kernel(ids, mine, other, master, up, flat, own, sem):
    @pl.when(ids[0] != 0)
    def _():
        copy = pltpu.make_async_copy(master.at[0 : own.shape[0]], own, sem)
        copy.start()

        @pl.when(ids[2] == 0)
        def _():
            flat[0:SHARE, :] = mine[...].astype(F32)
            flat[UP_LOW - SHARE : UP_LOW, :] = other[...].astype(F32)

        @pl.when(ids[2] != 0)
        def _():
            flat[0:SHARE, :] = other[...].astype(F32)
            flat[UP_LOW - SHARE : UP_LOW, :] = mine[...].astype(F32)

        copy.wait()
        flat[UP_LOW : UP_LOW + UP_HIGH, :] = own[0:UP_HIGH, :]
        for j in range(UP_N):
            up[j * D : (j + 1) * D, :] = flat[pl.ds(j, D, stride=UP_N), :].astype(BF)


def join(ids, mine, other, master):
    held = -(-UP_HIGH // 8) * 8
    return call(
        join_kernel,
        shaped(D * UP_N, LANE, BF),
        (
            pltpu.VMEM((D * UP_N, LANE), F32),
            pltpu.VMEM((held, LANE), F32),
            pltpu.SemaphoreType.DMA,
        ),
        in_specs=[SCALARS] + vm(2) + [WHOLE],
        out_specs=vm(1)[0],
        name="join",
    )(ids, mine, other, master)


def wide(ref, base, rows, first, count):
    return jnp.concatenate(
        [ref[base + j * rows : base + (j + 1) * rows, :] for j in range(first, first + count)],
        axis=1,
    )


def dot(left, right, dims=((1,), (0,))):
    return lax.dot_general(left, right, (dims, ((), ())), preferred_element_type=F32)


def times(left, ref, base, rows, blocks, finish):
    first = 0
    while first < blocks:
        count = min(2, blocks - first)
        finish(first * LANE, count * LANE, dot(left, wide(ref, base, rows, first, count)))
        first += count


def times_transposed(left, ref, base, rows, blocks):
    return dot(left, wide(ref, base, rows, 0, blocks), ((1,), (1,)))


def centred(hidden):
    centre = hidden - jnp.mean(hidden, axis=-1, keepdims=True)
    inv_std = lax.rsqrt(jnp.mean(centre * centre, axis=-1, keepdims=True) + ln_eps)
    return centre * inv_std, inv_std


def centred_backward(scaled, normed, inv_std):
    return inv_std * (
        scaled
        - jnp.mean(scaled, axis=-1, keepdims=True)
        - normed * jnp.mean(scaled * normed, axis=-1, keepdims=True)
    )


def key_mask(recv, lengths, seq, seq_len):
    cols = lax.broadcasted_iota(jnp.int32, (seq_len, seq_len), 1)
    if seq == 0:
        return cols < lengths[0]
    return cols.astype(F32) < recv[seq_len : seq_len + 1, 0:1].astype(F32)


def softmax_parts(proj, rows, head, mask):
    left = head * HD
    q = proj[rows, left : left + HD]
    k = proj[rows, INNER + left : INNER + left + HD]
    v = proj[rows, 2 * INNER + left : 2 * INNER + left + HD]
    scores = dot(q, k, ((1,), (1,))) * (1.0 / math.sqrt(HD))
    expd = jnp.where(mask, jnp.exp(scores), 0.0)
    exact = expd / jnp.sum(expd, axis=-1, keepdims=True)
    return q, k, v, exact


def attend_kernel(ids, lengths, tokens, recv, main, vec, normed, proj, ctx, xhat, rstd, hidden):
    seq_len = tokens.shape[0]

    @pl.when(ids[0] == 0)
    def _():
        both = jnp.concatenate([tokens[...], recv[0:seq_len, :]], axis=0)

        def keep(col, width, product):
            proj[:, col : col + width] = (product + vec[0:1, col : col + width]).astype(BF)

        times(both, main, 0, D, QKV_N, keep)
        for seq in range(2):
            rows = slice(seq * seq_len, (seq + 1) * seq_len)
            mask = key_mask(recv, lengths, seq, seq_len)
            for head in range(HEADS):
                _, _, v, exact = softmax_parts(proj, rows, head, mask)
                ctx[rows, head * HD : (head + 1) * HD] = dot(exact.astype(BF), v).astype(BF)

        def residual(col, width, product):
            cols = slice(col, col + width)
            hidden[:, cols] = both[:, cols].astype(F32) + product + vec[1:2, cols]

        times(ctx[...], main, QKV_N * D, INNER, DIM_N, residual)
        unit, inv_std = centred(hidden[...])
        xhat[...] = unit
        rstd[...] = jnp.broadcast_to(inv_std, rstd.shape)
        normed[...] = (unit * vec[2:3, 0:D] + vec[3:4, 0:D]).astype(BF)


def attend(ids, lengths, tokens, recv, main, vec):
    rows = 2 * tokens.shape[0]
    return call(
        attend_kernel,
        (
            shaped(rows, D, BF),
            shaped(rows, 3 * INNER, BF),
            shaped(rows, INNER, BF),
            shaped(rows, D, F32),
            shaped(rows, LANE, F32),
        ),
        (pltpu.VMEM((rows, D), F32),),
        in_specs=[SCALARS, SCALARS] + vm(4),
        out_specs=tuple(vm(5)),
        name="attend",
    )(ids, lengths, tokens, recv, main, vec)


def feed_kernel(
    ids, normed, cot, recv, up, main, vec, dnormed, dpre, act, dtwo, out, sums, pre, hidden
):
    seq_len = cot.shape[0]

    @pl.when(ids[0] != 0)
    def _():
        def activate(col, width, product):
            cols = slice(col, col + width)
            value = product + vec[0:1, cols]
            pre[:, cols] = value
            act[:, cols] = gelu_exact(value).astype(BF)

        source = normed[...]
        times(source, up, 0, D, UP_N, activate)

        def residual(col, width, product):
            cols = slice(col, col + width)
            hidden[:, cols] = source[:, cols].astype(F32) + product + vec[1:2, cols]

        times(act[...], main, 0, FF, DIM_N, residual)
        unit, inv_std = centred(hidden[...])
        gain = vec[2:3, 0:D]
        out[...] = (unit * gain + vec[3:4, 0:D]).astype(BF)
        grad = jnp.concatenate([recv[0:seq_len, :], cot[...]], axis=0).astype(F32)
        sums[2:3, 0:D] = jnp.sum(grad * unit, axis=0, keepdims=True)
        sums[3:4, 0:D] = jnp.sum(grad, axis=0, keepdims=True)
        d_two = centred_backward(grad * gain, unit, inv_std)
        sums[1:2, 0:D] = jnp.sum(d_two, axis=0, keepdims=True)
        hidden[...] = d_two
        dtwo[...] = d_two.astype(BF)
        half = dtwo[...]
        step = 2 * LANE
        for col in range(0, FF, step):
            cols = slice(col, col + step)
            rows = jnp.concatenate(
                [main[j * FF + col : j * FF + col + step, :] for j in range(DIM_N)], axis=1
            )
            d_pre = dot(half, rows, ((1,), (1,))) * gelu_slope(pre[:, cols])
            sums[0:1, cols] = jnp.sum(d_pre, axis=0, keepdims=True)
            dpre[:, cols] = d_pre.astype(BF)
        dnormed[...] = (hidden[...] + times_transposed(dpre[...], up, 0, D, UP_N)).astype(BF)


def feed(ids, normed, cot, recv, up, main, vec):
    rows = 2 * cot.shape[0]
    return call(
        feed_kernel,
        (
            shaped(rows, D, BF),
            shaped(rows, FF, BF),
            shaped(rows, FF, BF),
            shaped(rows, D, BF),
            shaped(rows, D, BF),
            shaped(8, FF, F32),
        ),
        (pltpu.VMEM((rows, FF), F32), pltpu.VMEM((rows, D), F32)),
        in_specs=[SCALARS] + vm(6),
        out_specs=tuple(vm(6)),
        name="feed",
    )(ids, normed, cot, recv, up, main, vec)


def attend_back_kernel(
    ids, lengths, dnormed, recv, proj, xhat, rstd, main, vec, dproj, done, gtok, sums
):
    seq_len = dnormed.shape[0] // 2

    @pl.when(ids[0] == 0)
    def _():
        grad = dnormed[...].astype(F32)
        unit = xhat[...]
        sums[2:3, 0:D] = jnp.sum(grad * unit, axis=0, keepdims=True)
        sums[3:4, 0:D] = jnp.sum(grad, axis=0, keepdims=True)
        d_one = centred_backward(grad * vec[2:3, 0:D], unit, rstd[:, 0:1])
        sums[1:2, 0:D] = jnp.sum(d_one, axis=0, keepdims=True)
        done[...] = d_one.astype(BF)
        dctx = times_transposed(done[...], main, QKV_N * D, INNER, DIM_N).astype(BF)
        totals = [[], []]
        for seq in range(2):
            rows = slice(seq * seq_len, (seq + 1) * seq_len)
            mask = key_mask(recv, lengths, seq, seq_len)
            for head in range(HEADS):
                q, k, v, exact = softmax_parts(proj, rows, head, mask)
                left = head * HD
                upper = dctx[rows, left : left + HD]
                d_probs = dot(upper, v, ((1,), (1,)))
                inner = jnp.sum(exact * d_probs, axis=-1, keepdims=True)
                d_scores = (exact * (d_probs - inner) * (1.0 / math.sqrt(HD))).astype(BF)
                d_q = dot(d_scores, k)
                d_k = dot(d_scores, q, ((0,), (0,)))
                d_v = dot(exact.astype(BF), upper, ((0,), (0,)))
                dproj[rows, left : left + HD] = d_q.astype(BF)
                dproj[rows, INNER + left : INNER + left + HD] = d_k.astype(BF)
                dproj[rows, 2 * INNER + left : 2 * INNER + left + HD] = d_v.astype(BF)
                totals[seq].append(
                    (jnp.sum(d_q, axis=0, keepdims=True), jnp.sum(d_v, axis=0, keepdims=True))
                )
        for head in range(HEADS):
            for part in range(2):
                left = part * INNER + head * HD
                sums[0:1, left : left + HD] = totals[0][head][part] + totals[1][head][part]
        gtok[...] = (d_one + times_transposed(dproj[...], main, 0, D, QKV_N)).astype(BF)


def attend_back(ids, lengths, dnormed, recv, proj, xhat, rstd, main, vec):
    rows = dnormed.shape[0]
    return call(
        attend_back_kernel,
        (
            shaped(rows, 3 * INNER, BF),
            shaped(rows, D, BF),
            shaped(rows, D, BF),
            shaped(8, FF, F32),
        ),
        in_specs=[SCALARS, SCALARS] + vm(7),
        out_specs=tuple(vm(4)),
        name="attend_back",
    )(ids, lengths, dnormed, recv, proj, xhat, rstd, main, vec)


def spread(flat, base, count, left, right):
    first = 0
    while first < count:
        step = min(2, count - first)
        block = dot(left, right[:, first * LANE : (first + step) * LANE], ((0,), (0,)))
        for j in range(step):
            flat[pl.ds(base + first + j, block.shape[0], stride=count), :] = block[
                :, j * LANE : (j + 1) * LANE
            ]
        first += step


def put_lines(flat, base, sums, row, count, start=0):
    for piece in range(count):
        flat[base + piece : base + piece + 1, :] = sums[
            row : row + 1, (start + piece) * LANE : (start + piece + 1) * LANE
        ]


def emit(ids, flat, base, pieces, unit, keep, send):
    for place in range(pieces):
        source = pl.multiple_of(base + ids[3 + place] * unit, 8)
        target = keep if place < pieces // 2 else send
        row = (place % (pieces // 2)) * unit
        target[row : row + unit, :] = flat[pl.ds(source, unit), :].astype(BF)


PAD = 8


def early_kernel(
    pieces, ids, tokens, recv, dproj, ctx, done, normed, dpre, act, dtwo, low, high, *rest
):
    outs, carry, flat = rest[: 2 * (CHUNKS - 1)], rest[-2], rest[-1]
    seq_len = tokens.shape[0]
    edge = outs[0].shape[0] * 2 * (CHUNKS - 1)

    @pl.when(ids[0] == 0)
    def _():
        both = jnp.concatenate([tokens[...], recv[0:seq_len, :]], axis=0)
        spread(flat, PAD, QKV_N, both, dproj[...])
        put_lines(flat, PAD + AT_BQV, low, 0, lines(2 * INNER))
        spread(flat, PAD + AT_OUT, DIM_N, ctx[...], done[...])

    @pl.when(ids[0] != 0)
    def _():
        cut = UP_LOW // UP_N
        spread(flat, PAD + cut * UP_N - UP_LOW, UP_N, normed[:, cut:D], dpre[...])
        put_lines(flat, PAD + AT_BUP - HALF, high, 0, UP_N)
        spread(flat, PAD + AT_DOWN - HALF, DIM_N, act[:, 0 : FF // 2], dtwo[...])

    unit = edge // ((CHUNKS - 1) * pieces)
    for chunk in range(CHUNKS - 1):
        emit(
            ids, flat, PAD + chunk * pieces * unit, pieces, unit, outs[2 * chunk], outs[2 * chunk + 1]
        )
    carry[...] = flat[PAD + edge : PAD + edge + carry.shape[0], :]


def late_kernel(pieces, ids, normed, dpre, act, dtwo, carry, low, high, keep, send, rest, flat):
    edge = 2 * keep.shape[0] * (CHUNKS - 1)
    flat[0 : carry.shape[0], :] = carry[...]

    @pl.when(ids[0] == 0)
    def _():
        put_lines(flat, AT_BOUT - edge, low, 1, DIM_N)
        put_lines(flat, AT_GONE - edge, low, 2, DIM_N)
        put_lines(flat, AT_BONE - edge, low, 3, DIM_N)
        cut = -(-UP_LOW // (UP_N * 8)) * 8
        spread(flat, AT_UP - edge, UP_N, normed[:, 0 : cut], dpre[...])

    @pl.when(ids[0] != 0)
    def _():
        spread(
            flat, AT_DOWN - HALF + FF // 2 * DIM_N - edge, DIM_N, act[:, FF // 2 : FF], dtwo[...]
        )
        put_lines(flat, AT_BDOWN - HALF - edge, high, 1, DIM_N)
        put_lines(flat, AT_GTWO - HALF - edge, high, 2, DIM_N)
        put_lines(flat, AT_BTWO - HALF - edge, high, 3, DIM_N)

    emit(ids, flat, 0, pieces, 2 * keep.shape[0] // pieces, keep, send)
    rest[...] = flat[2 * keep.shape[0] : 2 * keep.shape[0] + rest.shape[0], :].astype(BF)


def update_kernel(scale, halves, count, *refs):
    table, near, far = refs[0], refs[1], refs[2]
    refs = refs[3:]
    if count > halves * 2:
        extra, refs = refs[0], refs[1:]
    master, one, two = refs[:3]
    grad_out, master_out, one_out, two_out = refs[-4:]
    step = pl.program_id(0)

    def apply(source):
        gradient = source[...].astype(F32) * scale
        corr_one = 1.0 - beta_one**adam_step
        corr_two = 1.0 - beta_two**adam_step
        moment = beta_one * one[...] + (1.0 - beta_one) * gradient
        second = beta_two * two[...] + (1.0 - beta_two) * gradient * gradient
        held = master[...]
        step_dir = moment / corr_one / (jnp.sqrt(second / corr_two) + adam_eps)
        grad_out[...] = gradient
        one_out[...] = moment
        two_out[...] = second
        master_out[...] = held - learn_rate * (step_dir + decay_rate * held)

    pl.when(step < halves)(lambda: apply(near))
    pl.when((step >= halves) & (step < 2 * halves))(lambda: apply(far))
    if count > halves * 2:
        pl.when(step >= 2 * halves)(lambda: apply(extra))


def update(table, chunk, pieces, unit, near, far, extra, master, one, two, earlier, scale):
    halves = pieces // 2
    count = pieces + (extra is not None)
    base = chunk * pieces

    def place(step, table):
        inside = base + table[3 + jnp.minimum(step, pieces - 1)]
        return (jnp.where(step < pieces, inside, base + pieces), 0)

    block = pl.BlockSpec((unit, LANE), place)
    in_specs = [
        pl.BlockSpec((unit, LANE), lambda step, table: (jnp.minimum(step, halves - 1), 0)),
        pl.BlockSpec(
            (unit, LANE), lambda step, table: (jnp.clip(step - halves, 0, halves - 1), 0)
        ),
    ]
    args = [near, far]
    if extra is not None:
        in_specs.append(pl.BlockSpec((unit, LANE), lambda step, table: (0, 0)))
        args.append(extra)
    in_specs += [block] * 3
    args += [master, one, two]
    aliases = {}
    if earlier is not None:
        aliases = {1 + len(args) + i: i for i in range(4)}
        in_specs += [WHOLE] * 4
        args += list(earlier)
    return pl.pallas_call(
        partial(update_kernel, scale, halves, count),
        out_shape=tuple(jax.ShapeDtypeStruct(master.shape, F32) for _ in range(4)),
        grid_spec=pltpu.PrefetchScalarGridSpec(
            num_scalar_prefetch=1,
            grid=(count,),
            in_specs=in_specs,
            out_specs=tuple([block] * 4),
        ),
        input_output_aliases=aliases,
        name="update",
    )(table, *args)


def swap(value, axis, bit):
    size = lax.axis_size(axis)
    return lax.ppermute(value, axis, [(i, i ^ bit) for i in range(size)])


def added(left, right):
    return (left.astype(F32) + right.astype(F32)).astype(BF)


def per_device_pair(tokens, cotangent, lengths, master, moment_one, moment_two):
    seq_len = tokens.shape[0]
    dp_count = lax.axis_size("dp")
    half_id = lax.axis_index("zero")
    dp_id = lax.axis_index("dp")
    levels = dp_count.bit_length() - 1
    pieces = dp_count
    unit = HALF // (CHUNKS * pieces * 8) * 8
    first_half = half_id == 0
    order = [sum(((q >> b) & 1) << (levels - 1 - b) for b in range(levels)) for q in range(pieces)]
    ids = jnp.concatenate(
        [
            jnp.stack([half_id, dp_id, dp_id % 2]).astype(jnp.int32),
            (dp_id ^ jnp.array(order, jnp.int32)).astype(jnp.int32),
        ]
    )
    flat_master = master.reshape(HALF, LANE)

    payload = jnp.where(first_half, cotangent, tokens)
    marks = jnp.broadcast_to(lengths.astype(BF)[:, None], (8, D))
    recv = swap(jnp.concatenate([payload, marks], axis=0), "zero", 1)
    main, share, vec = prepare(ids, flat_master)
    near_share = swap(share, "zero", 1)
    far_share = swap(near_share, "dp", 1)
    normed, proj, ctx, xhat, rstd = attend(ids, lengths, tokens, recv, main, vec)
    normed_in = swap(normed, "zero", 1)
    up = join(ids, near_share, far_share, flat_master)
    dnormed, dpre, act, dtwo, out_rows, high = feed(ids, normed_in, cotangent, recv, up, main, vec)
    dnormed_in = swap(dnormed, "zero", 1)
    dpre_in = swap(dpre, "zero", 1)
    dproj, done, gtok, low = attend_back(ids, lengths, dnormed_in, recv, proj, xhat, rstd, main, vec)

    chunk_half = shaped(unit * pieces // 2, LANE, BF)
    *early, carry = call(
        partial(early_kernel, pieces),
        tuple([chunk_half] * (2 * (CHUNKS - 1)) + [shaped(16, LANE, F32)]),
        (pltpu.VMEM((PAD + unit * pieces * (CHUNKS - 1) + 24, LANE), F32),),
        in_specs=[SCALARS] + vm(11),
        out_specs=tuple(vm(2 * (CHUNKS - 1) + 1)),
        name="early",
    )(ids, tokens, recv, dproj, ctx, done, normed_in, dpre, act, dtwo, low, high)
    *late, extra = call(
        partial(late_kernel, pieces),
        (chunk_half, chunk_half, shaped(32, LANE, BF)),
        (pltpu.VMEM((unit * pieces + 128, LANE), F32),),
        in_specs=[SCALARS] + vm(7),
        out_specs=tuple(vm(3)),
        name="late",
    )(ids, normed, dpre_in, act, dtwo, carry, low, high)
    bufs = list(early) + list(late)

    reduced = []
    for chunk in range(CHUNKS):
        keep, send = bufs[2 * chunk], bufs[2 * chunk + 1]
        for level in range(levels):
            got = swap(send, "dp", 1 << level)
            if level < levels - 1:
                mid = keep.shape[0] // 2
                keep, send = added(keep[:mid], got[:mid]), added(keep[mid:], got[mid:])
            else:
                keep = added(keep, got)
        reduced.append(keep)
    for level in range(levels):
        extra = added(extra, swap(extra, "dp", 1 << level))

    seq_total = lengths.shape[0] * dp_count * lax.axis_size("zero")
    flats = [flat_master, moment_one.reshape(HALF, LANE), moment_two.reshape(HALF, LANE)]
    results = None
    for chunk in range(CHUNKS):
        held = reduced[chunk]
        for level in reversed(range(levels)):
            got = swap(held, "dp", 1 << level)
            if level:
                held = jnp.concatenate([held, got], axis=0)
        tail = None
        if chunk == CHUNKS - 1:
            tail = jnp.pad(extra, ((0, unit - extra.shape[0]), (0, 0)))
        results = update(
            ids, chunk, pieces, unit, held, got, tail, *flats, results, 1.0 / seq_total
        )
    gradient, master_new, moment_new, second_new = [item.reshape(-1) for item in results]

    back = swap(jnp.where(first_half, gtok[seq_len:], out_rows[:seq_len]), "zero", 1)
    out_mine = jnp.where(first_half, back, out_rows[seq_len:])
    grad_mine = jnp.where(first_half, gtok[:seq_len], back)
    return (out_mine, grad_mine, gradient, master_new, moment_new, second_new)


def pair_plan_fits(mesh):
    dp_count = mesh.shape["dp"]
    unit = HALF // (CHUNKS * dp_count * 8) * 8
    edge = unit * dp_count * (CHUNKS - 1)
    return (
        mesh.shape["zero"] == 2
        and dp_count > 1
        and dp_count & (dp_count - 1) == 0
        and HALF * 2 == TOTAL
        and 0 < HALF - CHUNKS * dp_count * unit <= 32
        and AT_OUT + lines(INNER * D) - 16 <= edge < AT_BOUT
    )


def per_device(tokens, cotangent, lengths, master, moment_one, moment_two, fits):
    if fits and lengths.shape[0] == 1 and master.shape[0] == HALF * LANE:
        return per_device_pair(tokens, cotangent, lengths, master, moment_one, moment_two)
    return per_device_general(tokens, cotangent, lengths, master, moment_one, moment_two)


def solution(mesh):
    placed = (
        P(("dp", "zero"), None),
        P(("dp", "zero"), None),
        P(("dp", "zero")),
        P("zero"),
        P("zero"),
        P("zero"),
    )
    return jax.shard_map(
        partial(per_device, fits=pair_plan_fits(mesh)),
        mesh=mesh,
        in_specs=placed,
        out_specs=(
            P(("dp", "zero"), None),
            P(("dp", "zero"), None),
            P("zero"),
            P("zero"),
            P("zero"),
            P("zero"),
        ),
        check_vma=False,
    )
```
